256 devices in a mesh: query: 4 (over y), cluster: 64 (over x, z, core).
Axes of the slice: x: 4, y: 4, z: 8, core: 2. Of those that a mesh axis runs over, the one named last changes fastest.
Arguments:
- queries: bfloat16 [1024, 512], P(('query', 'cluster')), may hold values from -68 to 68
- centroids: bfloat16 [512, 512], P('cluster'), may hold values from -6 to 6
- leaves: bfloat16 [512, 1024, 512], P('cluster'), may hold values from -5 to 5
- beam: int32 [1024, 8], P('query'), may hold values from 0 to 511, all different within a row; in each aligned block of 256 rows (0 to 255, 256 to 511, ...) at most 8 rows name the same one
Outputs:
- readout: bfloat16 [1024, 512], P(('query', 'cluster'))
- beam_logprob: float32 [1024, 8], P(('query', 'cluster'))
The draws below stay inside these ranges and needn't reach their ends.
Inputs may be any that keep to these rules, and one draw needn't show every extreme that they name: `beam`: each row names 8 different clusters. In each aligned block of 256 rows (the queries of one index of query) no cluster is named by more than 8 rows, a bound that some block reaches.
All inputs are finite; a program needn't handle non-finite values.
Results may differ from the reference program's by a relative error of at most 0.0028.
Values may be sent and summed in bfloat16 or wider, within the bound.
No kernel may reach another device: no remote copies, remote signals or barrier semaphores. Data moves between devices by JAX's collectives and lax.ppermute only.
A program may use at most 128 MiB of HBM per device.

```python
import math
import jax
import jax.numpy as jnp
import numpy as np
from jax import lax

D = 512
LEAF = 1024
TOP = 8
Q_DEV = 256
NCL = 512
NQ = 1024
CAP = 8


def draw_queries(key, part):
    second_key = jax.random.fold_in(jax.random.fold_in(key, 11), 1)
    base = jnp.clip(jax.random.normal(second_key, (NQ, D)), -5.0, 5.0)
    return (2.5 * base).astype(jnp.bfloat16)


def draw_leaves(key, part):
    first_key = jax.random.fold_in(jax.random.fold_in(key, 23), 0)
    base = jnp.clip(jax.random.normal(first_key, (NCL, LEAF, D)), -5.0, 5.0)
    return base.astype(jnp.bfloat16)


def level_of(rng, dims, pieces, least, largest):
    level = 1.0
    for dim, parts in pieces:
        heights = jax.random.uniform(jax.random.fold_in(jax.random.fold_in(rng, 6), dim), (parts,), jnp.float32, least / len(pieces), largest / len(pieces))
        level = level * jnp.repeat(jnp.exp(heights), dims[dim] // parts).reshape((-1,) + (1,) * (len(dims) - 1 - dim))
    return level


def assign_block(rng, own, number, rows, count, top, reach, slope):
    ranking = jax.random.permutation(rng, count)
    crowded, ordinary = load_shares(count, rows * top, reach, slope, True), load_shares(count, rows * top, reach, slope, False)
    places = jnp.arange(count)

    def named(tallies, offset_by):
        used = int((tallies > 0).sum())
        fixed = max(1, used // 4)
        shifted = fixed + (places - fixed + offset_by * (used - fixed)) % max(1, count - fixed)
        return jnp.zeros((count,), jnp.int32).at[ranking[jnp.where(places < fixed, places, shifted)]].set(jnp.asarray(tallies, jnp.int32))

    tallies = jnp.where(number % 4 == 0, named(crowded, number // 4), named(ordinary, number - number // 4 - 1))
    mixed = jax.random.permutation(jax.random.fold_in(own, 3), count)
    source_of, sink = mixed[0:count // 2 * 2:2], mixed[1:count // 2 * 2:2]
    room = jnp.minimum(tallies[source_of] - 1, reach - tallies[sink]) // 2
    room = jnp.where((source_of == ranking[0]) | (sink == ranking[0]) | (tallies[sink] == 0), 0, jnp.maximum(room, 0))
    shifted = jax.random.randint(jax.random.fold_in(own, 4), (count // 2,), 0, 1 << 20) % (room + 1)
    tallies = tallies.at[source_of].add(-shifted).at[sink].add(shifted)
    members = jnp.searchsorted(jnp.cumsum(tallies), jnp.arange(rows * top), side="right").astype(jnp.int32)
    listing = members.reshape(top, rows).T
    listing = listing[jax.random.permutation(jax.random.fold_in(own, 1), rows)]
    offset_by = jax.random.randint(jax.random.fold_in(own, 2), (rows, 1), 0, top)
    return jnp.take_along_axis(listing, (jnp.arange(top)[None, :] + offset_by) % top, axis=1)


def load_shares(number_of, total, bound, slope, full):
    weights = [(1 << 20) // math.isqrt(grade ** slope) + 1 for grade in range(1, number_of + 1)]
    largest = bound if full else min(bound, max(-(-total // number_of), total * weights[0] // sum(weights)))
    least = 1 if total - largest >= number_of - 1 else 0
    counts, surplus = [largest] + [least] * (number_of - 1), total - largest - least * (number_of - 1)
    while surplus > 0:
        candidates = [i for i in range(1, number_of) if counts[i] < largest] or [i for i in range(1, number_of) if counts[i] < bound]
        mass, left = sum([weights[i] for i in candidates]), surplus
        for i in candidates:
            more = min(bound - counts[i], max(1, left * weights[i] // mass), surplus)
            counts[i] = counts[i] + more
            surplus = surplus - more
    return np.array(counts)


def gaussian(rng, dims, deviation, most, shards=(), held_as=jnp.bfloat16):
    factor_of = level_of(rng, dims, shards, -0.22, 0.18) if shards else 1.0
    array = jax.random.normal(rng, dims, jnp.float32) * deviation * factor_of
    return jnp.minimum(jnp.maximum(array, -most), most).astype(held_as)


def setup_inputs(seed: int = 0) -> dict:
    arg_keys = jax.random.split(jax.random.key(seed), 5)
    queries = draw_queries(jax.random.fold_in(arg_keys[4], 71), 0)
    centroids = gaussian(arg_keys[1], (NCL, D), 1.0, 6.0, ((0, 64),))
    leaves = draw_leaves(jax.random.fold_in(arg_keys[4], 71), 0)
    beam_keys = jax.random.split(jax.random.fold_in(arg_keys[3], 1), NQ // Q_DEV)
    beam_turns = jax.random.permutation(jax.random.fold_in(arg_keys[3], 3), NQ // Q_DEV)
    beam = jax.vmap(lambda own, number: assign_block(jax.random.fold_in(arg_keys[3], 2), own, number, Q_DEV, NCL, TOP, CAP, 2))(beam_keys, beam_turns).reshape((NQ, TOP))
    return dict(queries=queries, centroids=centroids, leaves=leaves, beam=beam)


def reference(queries, centroids, leaves, beam):
    score_scale = 1.0 / math.sqrt(D)
    cscore = jnp.dot(queries, centroids.T, preferred_element_type=jnp.float32) * score_scale
    cmax = lax.optimization_barrier(jnp.max(cscore, axis=1))
    lse = cmax + jnp.log(lax.optimization_barrier(jnp.sum(jnp.exp(cscore - cmax[:, None]), axis=1)))
    beam_score = jnp.take_along_axis(cscore, beam, axis=1)
    beam_logprob = beam_score - lse[:, None]

    def one_block(packed):
        query_block, beam_block, score_block = packed
        gathered = leaves[beam_block].astype(jnp.float32)
        logits = jnp.einsum('qd,qkjd->qkj', query_block.astype(jnp.float32), gathered) * score_scale
        logits = logits + score_block[:, :, None]
        block_max = lax.optimization_barrier(jnp.max(logits, axis=2))
        weights = jnp.exp(logits - block_max[:, :, None])
        totals = lax.optimization_barrier(jnp.sum(weights, axis=2))
        rounded = weights.astype(jnp.bfloat16).astype(jnp.float32)
        accum = jnp.einsum('qkj,qkjd->qkd', rounded, gathered)
        overall = lax.optimization_barrier(jnp.max(block_max, axis=1))
        factor = jnp.exp(block_max - overall[:, None])
        numer = lax.optimization_barrier(jnp.sum(factor[:, :, None] * accum, axis=1))
        denom = lax.optimization_barrier(jnp.sum(factor * totals, axis=1))
        return (numer / denom[:, None]).astype(jnp.bfloat16)
    block_rows = 8
    packed = (queries.reshape(NQ // block_rows, block_rows, D), beam.reshape(NQ // block_rows, block_rows, TOP), beam_score.reshape(NQ // block_rows, block_rows, TOP))
    readout = lax.map(one_block, packed).reshape(NQ, D)
    return (readout, beam_logprob)
```

```python
import math

import jax
import jax.numpy as jnp
from jax import lax
from jax.sharding import PartitionSpec as P

floor_value = -1e30


def combine(first, second):
    m1, l1, a1 = first
    m2, l2, a2 = second
    m = jnp.maximum(m1, m2)
    f1 = jnp.exp(m1 - m)
    f2 = jnp.exp(m2 - m)
    return m, f1 * l1 + f2 * l2, f1 * a1 + f2 * a2


def per_device(queries, centroids, leaves, beam):
    groups = lax.axis_size("cluster")
    rows, width = queries.shape
    count, leaf_count, _ = leaves.shape
    top = beam.shape[1]
    pairs = groups // 2
    half = pairs * rows
    total = 2 * half
    scale = 1.0 / math.sqrt(width)
    me = lax.axis_index("cluster")
    side = me % 2
    sides = [[2 * i + c for i in range(pairs)] for c in range(2)]
    swap = [(i, i ^ 1) for i in range(groups)]

    own_q = lax.all_to_all(
        jnp.broadcast_to(queries[None], (pairs, rows, width)), "cluster", 0, 0, axis_index_groups=sides
    )
    other_q = lax.ppermute(own_q, "cluster", swap)
    q = jnp.concatenate([own_q, other_q], axis=0).reshape(total, width)
    beams = beam.reshape(pairs, 2, rows, top)
    b0 = beams[:, 0].reshape(half, top)
    b1 = beams[:, 1].reshape(half, top)
    own_beam = jnp.where(side == 0, b0, b1)
    b = jnp.concatenate([own_beam, jnp.where(side == 0, b1, b0)], axis=0)

    cscore = jnp.dot(q, centroids.T, preferred_element_type=jnp.float32) * scale
    owned = me * count + jnp.arange(count, dtype=jnp.int32)
    member = jnp.any(b[:, :, None] == owned[None, None, :], axis=1)
    rank = jnp.dot(
        jnp.tril(jnp.ones((total, total), jnp.bfloat16)),
        member.astype(jnp.bfloat16),
        preferred_element_type=jnp.float32,
    )
    capacity = 8
    slots = jnp.arange(1, capacity + 1, dtype=jnp.float32)
    dispatch = member.T[:, None, :] & (rank.T[:, None, :] == slots[None, :, None])
    picked = jnp.einsum(
        "csq,qd->csd", dispatch.astype(jnp.bfloat16), q, preferred_element_type=jnp.float32
    ).astype(jnp.bfloat16)
    slot_c = jnp.sum(jnp.where(dispatch, cscore.T[:, None, :], 0.0), axis=2)
    logits = jnp.einsum("csd,cjd->csj", picked, leaves, preferred_element_type=jnp.float32) * scale
    logits = logits + slot_c[:, :, None]
    slot_m = jnp.max(logits, axis=2)
    w = jnp.exp(logits - slot_m[:, :, None])
    slot_l = jnp.sum(w, axis=2)
    slot_a = jnp.einsum(
        "csj,cjd->csd", w.astype(jnp.bfloat16), leaves, preferred_element_type=jnp.float32
    )
    n = count * capacity
    d2 = dispatch.reshape(n, total)
    mm = slot_m.reshape(n, 1)
    m = jnp.max(jnp.where(d2, mm, floor_value), axis=0)
    f = jnp.where(d2, jnp.exp(jnp.where(d2, mm - m[None, :], 0.0)), 0.0)
    l = jnp.sum(f * slot_l.reshape(n, 1), axis=0)
    acc = lax.dot_general(
        f,
        slot_a.reshape(n, width),
        (((0,), (0,)), ((), ())),
        precision=lax.Precision.HIGHEST,
        preferred_element_type=jnp.float32,
    )
    pad = jnp.zeros((total, 128 - count - 2), jnp.float32)
    state = jnp.concatenate([acc, m[:, None], l[:, None], cscore, pad], axis=1)
    mine, theirs = state[:half], lax.ppermute(state[half:], "cluster", swap)

    def parts(s):
        return s[:, width : width + 1], s[:, width + 1 : width + 2], s[:, :width]

    m, l, acc = combine(parts(mine), parts(theirs))
    cs = slice(width + 2, width + 2 + count)
    pad = jnp.zeros((half, 128 - 2 * count - 2), jnp.float32)
    state = jnp.concatenate([acc, m, l, mine[:, cs], theirs[:, cs], pad], axis=1)
    got = lax.all_to_all(
        state.reshape(pairs, rows, width + 128), "cluster", 0, 0, axis_index_groups=sides
    )
    acc, m, l = got[:, :, :width], got[:, :, width], got[:, :, width + 1]
    scores = got[:, :, width + 2 : width + 2 + 2 * count]
    top_m = jnp.max(m, axis=0)
    f = jnp.exp(m - top_m[None])
    readout = jnp.sum(f[:, :, None] * acc, axis=0) / jnp.sum(f * l, axis=0)[:, None]
    cmax = jnp.max(scores, axis=(0, 2))
    lse = cmax + jnp.log(jnp.sum(jnp.exp(scores - cmax[None, :, None]), axis=(0, 2)))
    j = jnp.arange(2 * count, dtype=jnp.int32)
    from_side = jnp.where(j < count, side, 1 - side)
    ids = (2 * jnp.arange(pairs, dtype=jnp.int32)[:, None] + from_side[None]) * count + j[None] % count
    chip = me // 2
    my_beam = lax.dynamic_slice_in_dim(own_beam, chip * rows, rows, 0)
    hit = my_beam[None, :, :, None] == ids[:, None, None, :]
    picked_score = jnp.sum(jnp.where(hit, scores[:, :, None, :], 0.0), axis=(0, 3))
    return readout.astype(jnp.bfloat16), picked_score - lse[:, None]


def solution(mesh):
    return jax.shard_map(
        per_device,
        mesh=mesh,
        in_specs=(
            P(("query", "cluster"), None),
            P("cluster", None),
            P("cluster", None, None),
            P("query", None),
        ),
        out_specs=(P(("query", "cluster"), None), P(("query", "cluster"), None)),
        check_vma=False,
    )
```

```python
import functools
import math

import jax
import jax.numpy as jnp
from jax import lax
from jax.experimental import pallas as pl
from jax.experimental.pallas import tpu as pltpu
from jax.sharding import PartitionSpec as P

FLOOR = -1e30
CAP = 8
AHEAD = 2
LANES = 128
F32 = jnp.float32
BF16 = jnp.bfloat16


def dot(a, b, ca, cb):
    return lax.dot_general(a, b, (((ca,), (cb,)), ((), ())), preferred_element_type=F32)


def pieces(x):
    hi = x.astype(BF16)
    lo = (x - hi.astype(F32)).astype(BF16)
    return hi, lo


def table_kernel(beam_ref, cent_ref, leaves_ref, disp_ref, disp_t_ref, turned_ref, cent_out, head_out, beam_buf, sems):
    count = cent_ref.shape[0]
    total = beam_ref.shape[1]
    half = total // 2
    rows = total // lax.axis_size("cluster")
    ahead = head_out.shape[0]
    copies = [
        pltpu.make_async_copy(beam_ref, beam_buf, sems.at[0]),
        pltpu.make_async_copy(cent_ref, cent_out, sems.at[1]),
    ] + [pltpu.make_async_copy(leaves_ref.at[c], head_out.at[c], sems.at[2 + c]) for c in range(ahead)]
    for copy in copies:
        copy.start()
    me = lax.axis_index("cluster")
    square = (total, total)
    down, across = (lax.broadcasted_iota(jnp.int32, square, d) for d in range(2))
    upper = jnp.where(down <= across, 1.0, 0.0).astype(BF16)
    r = lax.broadcasted_iota(jnp.int32, (total, 1), 0)
    p, r = r // half, r % half
    source = (r // rows * 2 + (p + me) % 2) * rows + r % rows
    order = jnp.where(source == across, 1.0, 0.0).astype(BF16)
    copies[0].wait()
    beam = beam_buf[...]
    hits = [jnp.max(jnp.where(beam == me * count + c, 1.0, 0.0), axis=0, keepdims=True) for c in range(count)]
    rank = dot(jnp.concatenate(hits, axis=0).astype(BF16), upper, 1, 0)
    slot = lax.broadcasted_iota(jnp.int32, (CAP, total), 0).astype(F32) + 1.0
    disp = jnp.concatenate(
        [jnp.where(slot == rank[c : c + 1], 1.0, 0.0) * hits[c] for c in range(count)], axis=0
    ).astype(BF16)
    disp_ref[...] = dot(disp, order, 1, 1).astype(BF16)
    disp_t_ref[...] = dot(order, disp, 1, 1).astype(BF16)
    coarse = beam // 16 * 16
    halves = jnp.concatenate([coarse, beam - coarse], axis=0).astype(F32).astype(BF16)
    halves = dot(halves, order, 1, 1)
    top = beam.shape[0]
    turned_ref[...] = (halves[:top] + halves[top:]).astype(jnp.int32)
    for copy in copies[1:]:
        copy.wait()


def leaf_kernel(scale, own_ref, other_ref, disp_ref, disp_t_ref, beam_ref, cent_ref, head_ref, leaves_ref, mine_ref, theirs_ref, buf, sems):
    count, leaf_count, width = leaves_ref.shape
    ahead = head_ref.shape[0]
    half = own_ref.shape[0]
    total = 2 * half
    copies = [
        pltpu.make_async_copy(leaves_ref.at[ahead + c], buf.at[c], sems.at[c]) for c in range(count - ahead)
    ]
    for copy in copies:
        copy.start()
    q = jnp.concatenate([own_ref[...], other_ref[...]], axis=0)
    disp = disp_ref[...]
    picked = dot(disp, q, 1, 0).astype(BF16)
    cs = dot(cent_ref[...], q, 1, 1) * scale
    hit = disp.astype(F32)
    cs_wide = jnp.concatenate([jnp.broadcast_to(cs[c : c + 1], (CAP, total)) for c in range(count)], axis=0)
    slot_c = jnp.sum(hit * cs_wide, axis=1, keepdims=True)

    def leaf(c):
        return head_ref[c] if c < ahead else buf[c - ahead]

    def scores(c):
        if c >= ahead:
            copies[c - ahead].wait()
        return dot(picked[c * CAP : (c + 1) * CAP], leaf(c), 1, 1)

    ms, ls, accs = [], [], []
    s = scores(0)
    for c in range(count):
        z = s * scale + slot_c[c * CAP : (c + 1) * CAP]
        if c + 1 < count:
            s = scores(c + 1)
        m = jnp.max(z, axis=1, keepdims=True)
        w = jnp.exp(z - m)
        ms.append(m)
        ls.append(jnp.sum(w, axis=1, keepdims=True))
        accs.append(dot(w.astype(BF16), leaf(c), 1, 0))
    c_m = jnp.max(cs, axis=0, keepdims=True)
    c_l = jnp.sum(jnp.exp(cs - c_m), axis=0, keepdims=True)
    first = lax.axis_index("cluster") * count
    beam = beam_ref[...]
    score = jnp.zeros(beam.shape, F32)
    for c in range(count):
        score = score + jnp.where(beam == first + c, cs[c : c + 1], 0.0)
    m = jnp.concatenate(ms, axis=0)
    l = jnp.concatenate(ls, axis=0)
    acc = jnp.concatenate(accs, axis=0)
    on = hit > 0.5
    q_m = jnp.max(jnp.where(on, m, FLOOR), axis=0, keepdims=True)
    back = jnp.sum(jnp.where(on, q_m, 0.0), axis=1, keepdims=True)
    f = jnp.exp(jnp.minimum(m - back, 0.0))
    q_l = jnp.sum(jnp.where(on, f * l, 0.0), axis=0, keepdims=True)
    hi, lo = pieces(f * acc)
    disp_t = disp_t_ref[...]
    q_acc = dot(disp_t, hi, 1, 0) + dot(disp_t, lo, 1, 0)
    rows = jnp.concatenate([q_m, q_l, c_m, c_l, score, jnp.zeros((4, total), F32)], axis=0)
    for side, ref in enumerate((mine_ref, theirs_ref)):
        for k in range(width // LANES):
            ref[k * half : (k + 1) * half] = q_acc[side * half : (side + 1) * half, k * LANES : (k + 1) * LANES]
        ref[width // LANES * half :] = rows[:, side * half : (side + 1) * half]


def merge_kernel(mine_ref, theirs_ref, out_ref):
    chunks = (mine_ref.shape[0] - 16) // LANES
    half = LANES
    base = chunks * half
    a, b = mine_ref[base : base + 16], theirs_ref[base : base + 16]
    m = jnp.maximum(a[0:1], b[0:1])
    fa, fb = jnp.exp(a[0:1] - m), jnp.exp(b[0:1] - m)
    l = fa * a[1:2] + fb * b[1:2]
    c = jnp.maximum(a[2:3], b[2:3])
    cl = jnp.exp(a[2:3] - c) * a[3:4] + jnp.exp(b[2:3] - c) * b[3:4]
    block = jnp.concatenate([m, l, c, cl, a[4:12] + b[4:12], fa, fb, jnp.zeros((LANES - 14, half), F32)], axis=0)
    cols = block.T
    fa, fb = cols[:, 12:13], cols[:, 13:14]
    per = out_ref.shape[0] * 4 // half
    outs = [
        fa * mine_ref[k * half : (k + 1) * half] + fb * theirs_ref[k * half : (k + 1) * half] for k in range(chunks)
    ] + [cols]
    for k, value in enumerate(outs):
        for d in range(half // 4):
            out_ref[per * d + k] = value[4 * d : 4 * d + 4]


def home_kernel(got_ref, readout_ref, logprob_ref):
    rows, width = readout_ref.shape
    chunks = width // LANES
    per = chunks + 1
    pairs = got_ref.shape[0] // per
    info = [got_ref[per * d + chunks] for d in range(pairs)]
    top = functools.reduce(jnp.maximum, info)
    total = functools.reduce(jnp.add, info)
    factors = [jnp.exp(x - top) for x in info]
    sums = functools.reduce(jnp.add, [e * pltpu.roll(x, LANES - 1, 1) for e, x in zip(factors, info)])
    wide = [jnp.broadcast_to(e[:, 0:1], (rows, LANES)) for e in factors]
    inv = 1.0 / sums[:, 0:1]
    for k in range(chunks):
        acc = functools.reduce(jnp.add, [wide[d] * got_ref[per * d + k] for d in range(pairs)])
        readout_ref[:, k * LANES : (k + 1) * LANES] = (acc * inv).astype(BF16)
    logprob_ref[...] = total[:, 4:12] - (top[:, 2:3] + jnp.log(sums[:, 2:3]))


def per_device(queries, centroids, leaves, beam):
    groups = lax.axis_size("cluster")
    rows, width = queries.shape
    count, leaf_count, _ = leaves.shape
    top = beam.shape[1]
    pairs = groups // 2
    half = pairs * rows
    total = 2 * half
    scale = 1.0 / math.sqrt(width)
    me = lax.axis_index("cluster")
    side = me % 2
    sides = [[2 * i + c for i in range(pairs)] for c in range(2)]
    swap = [(i, i ^ 1) for i in range(groups)]
    vmem = pl.BlockSpec(memory_space=pltpu.VMEM)

    hbm = pl.BlockSpec(memory_space=pltpu.HBM)
    leaves, centroids = (pltpu.with_memory_space_constraint(a, pltpu.HBM) for a in (leaves, centroids))

    spread = jnp.broadcast_to(queries[None], (pairs, rows, width))
    own = lax.all_to_all(spread, "cluster", 0, 0, axis_index_groups=sides)
    own, beam = lax.optimization_barrier((own, beam))
    other = lax.ppermute(own, "cluster", swap)
    slots = count * CAP
    tables = pl.pallas_call(
        table_kernel,
        out_shape=(
            jax.ShapeDtypeStruct((slots, total), BF16),
            jax.ShapeDtypeStruct((total, slots), BF16),
            jax.ShapeDtypeStruct((top, total), jnp.int32),
            jax.ShapeDtypeStruct(centroids.shape, BF16),
            jax.ShapeDtypeStruct((AHEAD, leaf_count, width), BF16),
        ),
        in_specs=[hbm] * 3,
        out_specs=(vmem,) * 5,
        scratch_shapes=[pltpu.VMEM((top, total), jnp.int32), pltpu.SemaphoreType.DMA((2 + AHEAD,))],
        compiler_params=pltpu.CompilerParams(vmem_limit_bytes=4 << 20),
        cost_estimate=pl.CostEstimate(flops=50_000_000, bytes_accessed=4 << 20, transcendentals=0),
        name="table",
    )(pltpu.with_memory_space_constraint(beam.T, pltpu.HBM), centroids, leaves)
    state = jax.ShapeDtypeStruct((width // LANES * half + 16, LANES), F32)
    mine, theirs = pl.pallas_call(
        functools.partial(leaf_kernel, scale),
        out_shape=(state, state),
        in_specs=[vmem] * 7 + [hbm],
        out_specs=(vmem, vmem),
        scratch_shapes=[pltpu.VMEM((count - AHEAD, leaf_count, width), BF16), pltpu.SemaphoreType.DMA((count - AHEAD,))],
        compiler_params=pltpu.CompilerParams(vmem_limit_bytes=24 << 20),
        name="leaf",
    )(own.reshape(half, width), other.reshape(half, width), *tables, leaves)
    theirs = lax.ppermute(theirs, "cluster", swap)
    per = width // LANES + 1
    packed = pl.pallas_call(
        merge_kernel,
        out_shape=jax.ShapeDtypeStruct((pairs * per, rows, LANES), F32),
        in_specs=[vmem, vmem],
        out_specs=vmem,
        compiler_params=pltpu.CompilerParams(vmem_limit_bytes=8 << 20),
        name="merge",
    )(mine, theirs)
    got = lax.all_to_all(packed, "cluster", 0, 0, axis_index_groups=sides, tiled=True)
    return pl.pallas_call(
        home_kernel,
        out_shape=(jax.ShapeDtypeStruct((rows, width), BF16), jax.ShapeDtypeStruct((rows, top), F32)),
        in_specs=[vmem],
        out_specs=(vmem, vmem),
        compiler_params=pltpu.CompilerParams(vmem_limit_bytes=8 << 20),
        name="home",
    )(got)


def solution(mesh):
    return jax.shard_map(
        per_device,
        mesh=mesh,
        in_specs=(
            P(("query", "cluster"), None),
            P("cluster", None),
            P("cluster", None, None),
            P("query", None),
        ),
        out_specs=(P(("query", "cluster"), None), P(("query", "cluster"), None)),
        check_vma=False,
    )
```

```python
import functools
import math

import jax
import jax.numpy as jnp
from jax import lax
from jax.experimental import pallas as pl
from jax.experimental.pallas import tpu as pltpu
from jax.sharding import PartitionSpec as P

FLOOR = -30000.0
CAP = 8
AHEAD = 2
LANES = 128
F32 = jnp.float32
BF16 = jnp.bfloat16


def dot(a, b, ca, cb):
    return lax.dot_general(a, b, (((ca,), (cb,)), ((), ())), preferred_element_type=F32)


def pieces(x):
    hi = x.astype(BF16)
    lo = (x - hi.astype(F32)).astype(BF16)
    return hi, lo


def table_kernel(beam_ref, cent_ref, leaves_ref, disp_ref, disp_t_ref, turned_ref, cent_out, head_out, beam_buf, sems):
    count = cent_ref.shape[0]
    total = beam_ref.shape[1]
    half = total // 2
    rows = total // lax.axis_size("cluster")
    ahead = head_out.shape[0]
    copies = [
        pltpu.make_async_copy(beam_ref, beam_buf, sems.at[0]),
        pltpu.make_async_copy(cent_ref, cent_out, sems.at[1]),
    ] + [pltpu.make_async_copy(leaves_ref.at[c], head_out.at[c], sems.at[2 + c]) for c in range(ahead)]
    for copy in copies:
        copy.start()
    me = lax.axis_index("cluster")
    square = (total, total)
    down, across = (lax.broadcasted_iota(jnp.int32, square, d) for d in range(2))
    upper = jnp.where(down <= across, 1.0, 0.0).astype(BF16)
    r = lax.broadcasted_iota(jnp.int32, (total, 1), 0)
    p, r = r // half, r % half
    source = (r // rows * 2 + (p + me) % 2) * rows + r % rows
    order = jnp.where(source == across, 1.0, 0.0).astype(BF16)
    copies[0].wait()
    beam = beam_buf[...]
    hits = [jnp.max(jnp.where(beam == me * count + c, 1.0, 0.0), axis=0, keepdims=True) for c in range(count)]
    rank = dot(jnp.concatenate(hits, axis=0).astype(BF16), upper, 1, 0)
    slot = lax.broadcasted_iota(jnp.int32, (CAP, total), 0).astype(F32) + 1.0
    disp = jnp.concatenate(
        [jnp.where(slot == rank[c : c + 1], 1.0, 0.0) * hits[c] for c in range(count)], axis=0
    ).astype(BF16)
    disp_ref[...] = dot(disp, order, 1, 1).astype(BF16)
    disp_t_ref[...] = dot(order, jnp.concatenate([disp, disp], axis=0), 1, 1).astype(BF16)
    coarse = beam // 16 * 16
    halves = jnp.concatenate([coarse, beam - coarse], axis=0).astype(F32).astype(BF16)
    halves = dot(halves, order, 1, 1)
    top = beam.shape[0]
    turned_ref[...] = (halves[:top] + halves[top:]).astype(jnp.int32)
    for copy in copies[1:]:
        copy.wait()


def leaf_kernel(scale, own_ref, other_ref, disp_ref, disp_t_ref, beam_ref, cent_ref, head_ref, leaves_ref, mine_ref, theirs_ref, buf, sems):
    count, leaf_count, width = leaves_ref.shape
    ahead = head_ref.shape[0]
    half = own_ref.shape[0]
    total = 2 * half
    copies = [
        pltpu.make_async_copy(leaves_ref.at[ahead + c], buf.at[c], sems.at[c]) for c in range(count - ahead)
    ]
    for copy in copies:
        copy.start()
    q = jnp.concatenate([own_ref[...], other_ref[...]], axis=0)
    disp = disp_ref[...]
    picked = dot(disp, q, 1, 0).astype(BF16)
    cs = dot(cent_ref[...], q, 1, 1) * scale
    hit = disp.astype(F32)
    cs_wide = jnp.concatenate([jnp.broadcast_to(cs[c : c + 1], (CAP, total)) for c in range(count)], axis=0)
    slot_c = jnp.sum(hit * cs_wide, axis=1, keepdims=True)

    def leaf(c):
        return head_ref[c] if c < ahead else buf[c - ahead]

    def scores(c):
        if c >= ahead:
            copies[c - ahead].wait()
        return dot(picked[c * CAP : (c + 1) * CAP], leaf(c), 1, 1)

    ms, ls, accs = [], [], []
    s = scores(0)
    for c in range(count):
        z = s * scale + slot_c[c * CAP : (c + 1) * CAP]
        if c + 1 < count:
            s = scores(c + 1)
        m = jnp.max(z, axis=1, keepdims=True)
        w = jnp.exp(z - m)
        ms.append(m)
        ls.append(jnp.sum(w, axis=1, keepdims=True))
        accs.append(dot(w.astype(BF16), leaf(c), 1, 0))
    c_m = jnp.max(cs, axis=0, keepdims=True)
    c_l = jnp.sum(jnp.exp(cs - c_m), axis=0, keepdims=True)
    first = lax.axis_index("cluster") * count
    beam = beam_ref[...]
    score = jnp.zeros(beam.shape, F32)
    for c in range(count):
        score = score + jnp.where(beam == first + c, cs[c : c + 1], 0.0)
    m = jnp.concatenate(ms, axis=0)
    l = jnp.concatenate(ls, axis=0)
    acc = jnp.concatenate(accs, axis=0)
    on = hit > 0.5
    q_m = jnp.max(jnp.where(on, m, FLOOR), axis=0, keepdims=True)
    back = jnp.sum(jnp.where(on, q_m, 0.0), axis=1, keepdims=True)
    f = jnp.exp(jnp.minimum(m - back, 0.0))
    q_l = jnp.sum(jnp.where(on, f * l, 0.0), axis=0, keepdims=True)
    hi, lo = pieces(f * acc)
    q_acc = dot(disp_t_ref[...], jnp.concatenate([hi, lo], axis=0), 1, 0)
    rows = jnp.concatenate([q_m, q_l, c_m, c_l, score, jnp.zeros((4, total), F32)], axis=0)
    for side, ref in enumerate((mine_ref, theirs_ref)):
        for k in range(width // LANES):
            ref[k * half : (k + 1) * half] = q_acc[side * half : (side + 1) * half, k * LANES : (k + 1) * LANES]
        ref[width // LANES * half :] = rows[:, side * half : (side + 1) * half]


def merge_kernel(mine_ref, theirs_ref, out_ref):
    chunks = (mine_ref.shape[0] - 16) // LANES
    half = LANES
    base = chunks * half
    a, b = mine_ref[base : base + 16], theirs_ref[base : base + 16]
    m = jnp.maximum(a[0:1], b[0:1])
    fa, fb = jnp.exp(a[0:1] - m), jnp.exp(b[0:1] - m)
    l = fa * a[1:2] + fb * b[1:2]
    c = jnp.maximum(a[2:3], b[2:3])
    cl = jnp.exp(a[2:3] - c) * a[3:4] + jnp.exp(b[2:3] - c) * b[3:4]
    inv = 1.0 / jnp.maximum(l, 1e-30)
    info = jnp.concatenate([m, l, c, cl, a[4:12] + b[4:12], jnp.zeros((4, half), F32)], axis=0)
    hi = info.astype(BF16).astype(F32)
    rest = info - hi
    mid = rest.astype(BF16).astype(F32)
    block = jnp.concatenate(
        [hi, mid * 256.0, (rest - mid) * 65536.0, fa * inv, fb * inv, jnp.zeros((LANES - 50, half), F32)], axis=0
    )
    cols = block.T
    fa, fb = cols[:, 48:49], cols[:, 49:50]
    outs = [
        fa * mine_ref[k * half : (k + 1) * half] + fb * theirs_ref[k * half : (k + 1) * half] for k in range(chunks)
    ]
    high = jnp.max(functools.reduce(jnp.maximum, [jnp.abs(o) for o in outs]), axis=1, keepdims=True)
    power = jnp.floor(jnp.log2(jnp.maximum(high, 1e-30)))
    down = jnp.exp2(-power)
    lane = lax.broadcasted_iota(jnp.int32, (half, LANES), 1)
    cols = jnp.where(lane == 12, power, jnp.where(lane < 48, cols, 0.0))
    per = chunks + 1
    for k, value in enumerate([o * down for o in outs] + [cols]):
        for d in range(half // 4):
            out_ref[per * d + k] = value[4 * d : 4 * d + 4]


def home_kernel(got_ref, readout_ref, logprob_ref):
    rows, width = readout_ref.shape
    chunks = width // LANES
    per = chunks + 1
    pairs = got_ref.shape[0] // per
    info = jnp.concatenate([got_ref[per * d + chunks] for d in range(pairs)], axis=0)

    def left(x, n):
        return pltpu.roll(x, LANES - n, 1)

    info = info + left(info, 16) * (1.0 / 256.0) + left(info, 32) * (1.0 / 65536.0)
    tiles = [info[8 * t : 8 * t + 8] for t in range(pairs * rows // 8)]

    def fold(op, xs):
        x = functools.reduce(op, xs)
        return op(x, pltpu.roll(x, 4, 0))

    top = fold(jnp.maximum, tiles)
    total = fold(jnp.add, tiles)
    prods = [jnp.exp(x - top) * left(x, 1) for x in tiles]
    sums = fold(jnp.add, prods)
    coefs = [
        jnp.broadcast_to(p[:, 0:1] * jnp.exp2(x[:, 12:13]), (8, LANES)) for p, x in zip(prods, tiles)
    ]
    coefs = [coefs[d // 2][d % 2 * 4 : d % 2 * 4 + 4] for d in range(pairs)]
    inv = 1.0 / sums[:rows, 0:1]
    for k in range(chunks):
        acc = functools.reduce(jnp.add, [coefs[d] * got_ref[per * d + k] for d in range(pairs)])
        readout_ref[:, k * LANES : (k + 1) * LANES] = (acc * inv).astype(BF16)
    logprob_ref[...] = total[:rows, 4:12] - (top[:rows, 2:3] + jnp.log(sums[:rows, 2:3]))


def per_device(queries, centroids, leaves, beam):
    groups = lax.axis_size("cluster")
    rows, width = queries.shape
    count, leaf_count, _ = leaves.shape
    top = beam.shape[1]
    pairs = groups // 2
    half = pairs * rows
    total = 2 * half
    scale = 1.0 / math.sqrt(width)
    me = lax.axis_index("cluster")
    side = me % 2
    sides = [[2 * i + c for i in range(pairs)] for c in range(2)]
    swap = [(i, i ^ 1) for i in range(groups)]
    vmem = pl.BlockSpec(memory_space=pltpu.VMEM)

    hbm = pl.BlockSpec(memory_space=pltpu.HBM)
    leaves, centroids = (pltpu.with_memory_space_constraint(a, pltpu.HBM) for a in (leaves, centroids))

    spread = jnp.broadcast_to(queries[None], (pairs, rows, width))
    own = lax.all_to_all(spread, "cluster", 0, 0, axis_index_groups=sides)
    own, beam = lax.optimization_barrier((own, beam))
    other = lax.ppermute(own, "cluster", swap)
    slots = count * CAP
    tables = pl.pallas_call(
        table_kernel,
        out_shape=(
            jax.ShapeDtypeStruct((slots, total), BF16),
            jax.ShapeDtypeStruct((total, 2 * slots), BF16),
            jax.ShapeDtypeStruct((top, total), jnp.int32),
            jax.ShapeDtypeStruct(centroids.shape, BF16),
            jax.ShapeDtypeStruct((AHEAD, leaf_count, width), BF16),
        ),
        in_specs=[hbm] * 3,
        out_specs=(vmem,) * 5,
        scratch_shapes=[pltpu.VMEM((top, total), jnp.int32), pltpu.SemaphoreType.DMA((2 + AHEAD,))],
        compiler_params=pltpu.CompilerParams(vmem_limit_bytes=4 << 20),
        cost_estimate=pl.CostEstimate(flops=50_000_000, bytes_accessed=4 << 20, transcendentals=0),
        name="table",
    )(pltpu.with_memory_space_constraint(beam.T, pltpu.HBM), centroids, leaves)
    state = jax.ShapeDtypeStruct((width // LANES * half + 16, LANES), F32)
    mine, theirs = pl.pallas_call(
        functools.partial(leaf_kernel, scale),
        out_shape=(state, state),
        in_specs=[vmem] * 7 + [hbm],
        out_specs=(vmem, vmem),
        scratch_shapes=[pltpu.VMEM((count - AHEAD, leaf_count, width), BF16), pltpu.SemaphoreType.DMA((count - AHEAD,))],
        compiler_params=pltpu.CompilerParams(vmem_limit_bytes=24 << 20),
        name="leaf",
    )(own.reshape(half, width), other.reshape(half, width), *tables, leaves)
    theirs = lax.ppermute(theirs, "cluster", swap)
    per = width // LANES + 1
    packed = pl.pallas_call(
        merge_kernel,
        out_shape=jax.ShapeDtypeStruct((pairs * per, rows, LANES), F32),
        in_specs=[vmem, vmem],
        out_specs=vmem,
        compiler_params=pltpu.CompilerParams(vmem_limit_bytes=8 << 20),
        name="merge",
    )(mine, theirs)
    packed = packed.astype(jnp.float16)
    got = lax.all_to_all(packed, "cluster", 0, 0, axis_index_groups=sides, tiled=True).astype(F32)
    return pl.pallas_call(
        home_kernel,
        out_shape=(jax.ShapeDtypeStruct((rows, width), BF16), jax.ShapeDtypeStruct((rows, top), F32)),
        in_specs=[vmem],
        out_specs=(vmem, vmem),
        compiler_params=pltpu.CompilerParams(vmem_limit_bytes=8 << 20),
        name="home",
    )(got)


def solution(mesh):
    return jax.shard_map(
        per_device,
        mesh=mesh,
        in_specs=(
            P(("query", "cluster"), None),
            P("cluster", None),
            P("cluster", None, None),
            P("query", None),
        ),
        out_specs=(P(("query", "cluster"), None), P(("query", "cluster"), None)),
        check_vma=False,
    )
```

```python
import functools
import math

import jax
import jax.numpy as jnp
from jax import lax
from jax.experimental import pallas as pl
from jax.experimental.pallas import tpu as pltpu
from jax.sharding import PartitionSpec as P

FLOOR = -30000.0
CAP = 8
LANES = 128
F32 = jnp.float32
BF16 = jnp.bfloat16


def dot(a, b, ca, cb):
    return lax.dot_general(a, b, (((ca,), (cb,)), ((), ())), preferred_element_type=F32)


def pieces(x):
    hi = x.astype(BF16)
    lo = (x - hi.astype(F32)).astype(BF16)
    return hi, lo


def table_kernel(beam_ref, cent_ref, disp_ref, mine_ref, mine_t_ref, turned_ref, cent_out, beam_buf, sems):
    count = cent_ref.shape[0]
    total = beam_ref.shape[1]
    half = total // 2
    rows = total // lax.axis_size("cluster")
    copies = [
        pltpu.make_async_copy(beam_ref, beam_buf, sems.at[0]),
        pltpu.make_async_copy(cent_ref, cent_out, sems.at[1]),
    ]
    for copy in copies:
        copy.start()
    me = lax.axis_index("cluster")
    square = (total, total)
    down, across = (lax.broadcasted_iota(jnp.int32, square, d) for d in range(2))
    upper = jnp.where(down <= across, 1.0, 0.0).astype(BF16)
    r = lax.broadcasted_iota(jnp.int32, (total, 1), 0)
    p, r = r // half, r % half
    source = (r // rows * 2 + (p + me) % 2) * rows + r % rows
    order = jnp.where(source == across, 1.0, 0.0).astype(BF16)
    copies[0].wait()
    beam = beam_buf[...]
    firsts = ((me + 1 - 2 * (me % 2)) * count, me * count)
    hits = [
        jnp.max(jnp.where(beam == first + c, 1.0, 0.0), axis=0, keepdims=True) for first in firsts for c in range(count)
    ]
    rank = dot(jnp.concatenate(hits, axis=0).astype(BF16), upper, 1, 0)
    slot = lax.broadcasted_iota(jnp.int32, (CAP, total), 0).astype(F32) + 1.0
    disp = jnp.concatenate(
        [jnp.where(slot == rank[c : c + 1], 1.0, 0.0) * hits[c] for c in range(2 * count)], axis=0
    ).astype(BF16)
    turned = dot(disp, order, 1, 1).astype(BF16)
    disp_ref[...] = turned[: count * CAP]
    mine_ref[...] = turned[:, :half]
    mine_t_ref[...] = dot(order[:half], jnp.concatenate([disp, disp], axis=0), 1, 1).astype(BF16)
    coarse = beam // 16 * 16
    halves = jnp.concatenate([coarse, beam - coarse], axis=0).astype(F32).astype(BF16)
    halves = dot(halves, order[:half], 1, 1)
    top = beam.shape[0]
    turned_ref[...] = (halves[:top] + halves[top:]).astype(jnp.int32)
    copies[1].wait()


def leaf_kernel(scale, own_ref, other_ref, disp_ref, cent_ref, leaves_ref, pack_ref, info_ref, q_ref):
    count, leaf_count, width = leaves_ref.shape
    pairs, rows, _ = own_ref.shape
    half = pairs * rows
    total = 2 * half
    for side, ref in enumerate((own_ref, other_ref)):
        for d in range(pairs):
            q_ref[side * half + d * rows : side * half + (d + 1) * rows] = ref[d]
    q = q_ref[...]
    disp = disp_ref[...]
    picked = dot(disp, q, 1, 0).astype(BF16)
    cs = dot(cent_ref[...], q, 1, 1) * scale
    def scores(c):
        return dot(picked[c * CAP : (c + 1) * CAP], leaves_ref[c], 1, 1)

    ms, ls, accs = [], [], []
    s = scores(0)
    for c in range(count):
        z = s * scale
        if c + 1 < count:
            s = scores(c + 1)
        m = jnp.max(z, axis=1, keepdims=True)
        w = jnp.exp(z - m)
        ms.append(m)
        ls.append(jnp.sum(w, axis=1, keepdims=True))
        accs.append(dot(w.astype(BF16), leaves_ref[c], 1, 0))
    info_ref[...] = cs[:, :half]
    slots = count * CAP
    for c in range(count):
        for k in range(width // LANES):
            pack_ref[k * slots + c * CAP : k * slots + (c + 1) * CAP] = accs[c][:, k * LANES : (k + 1) * LANES]
    lane = lax.broadcasted_iota(jnp.int32, (slots, LANES), 1)
    base = width // LANES * slots
    pack_ref[base : base + slots] = jnp.where(
        lane == 0, jnp.concatenate(ms, axis=0), jnp.concatenate(ls, axis=0)
    )
    pack_ref[base + slots :] = cs[:, half:]


def merge_kernel(pack_ref, info_ref, theirs_ref, mine_ref, mine_t_ref, beam_ref, out_ref):
    half = info_ref.shape[1]
    slots = mine_ref.shape[0] // 2
    count = info_ref.shape[0]
    chunks = (pack_ref.shape[0] - count) // slots - 1
    base = chunks * slots

    def both(k):
        return jnp.concatenate([ref[k * slots : (k + 1) * slots] for ref in (pack_ref, theirs_ref)], axis=0)

    stats = both(chunks)
    cs = jnp.concatenate([theirs_ref[base + slots :], info_ref[...]], axis=0)
    wide = jnp.concatenate([jnp.broadcast_to(cs[c : c + 1], (CAP, half)) for c in range(2 * count)], axis=0)
    on = mine_ref[...].astype(F32) > 0.5
    slot_m = stats[:, 0:1] + jnp.sum(jnp.where(on, wide, 0.0), axis=1, keepdims=True)
    slot_l = stats[:, 1:2]
    m = jnp.max(jnp.where(on, slot_m, FLOOR), axis=0, keepdims=True)
    back = jnp.sum(jnp.where(on, m, 0.0), axis=1, keepdims=True)
    f = jnp.exp(jnp.minimum(slot_m - back, 0.0))
    l = jnp.sum(jnp.where(on, f * slot_l, 0.0), axis=0, keepdims=True)
    mine_t = mine_t_ref[...]
    accs = []
    for k in range(chunks):
        hi, lo = pieces(f * both(k))
        accs.append(dot(mine_t, jnp.concatenate([hi, lo], axis=0), 1, 0))
    c = jnp.max(cs, axis=0, keepdims=True)
    cl = jnp.sum(jnp.exp(cs - c), axis=0, keepdims=True)
    me = lax.axis_index("cluster")
    firsts = ((me + 1 - 2 * (me % 2)) * count, me * count)
    beam = beam_ref[...]
    score = jnp.zeros(beam.shape, F32)
    for i in range(2 * count):
        score = score + jnp.where(beam == firsts[i // count] + i % count, cs[i : i + 1], 0.0)
    inv = 1.0 / jnp.maximum(l, 1e-30)
    info = jnp.concatenate([m, l, c, cl, score, jnp.zeros((4, half), F32)], axis=0)
    hi = info.astype(BF16).astype(F32)
    rest = info - hi
    mid = rest.astype(BF16).astype(F32)
    block = jnp.concatenate(
        [hi, mid * 256.0, (rest - mid) * 65536.0, inv, jnp.zeros((LANES - 49, half), F32)], axis=0
    )
    cols = block.T
    inv = cols[:, 48:49]
    outs = [acc * inv for acc in accs]
    high = jnp.max(functools.reduce(jnp.maximum, [jnp.abs(o) for o in outs]), axis=1, keepdims=True)
    power = jnp.floor(jnp.log2(jnp.maximum(high, 1e-30)))
    down = jnp.exp2(-power)
    lane = lax.broadcasted_iota(jnp.int32, (half, LANES), 1)
    cols = jnp.where(lane == 12, power, jnp.where(lane < 48, cols, 0.0))
    per = chunks + 1
    for k, value in enumerate([o * down for o in outs] + [cols]):
        for d in range(half // 4):
            out_ref[per * d + k] = value[4 * d : 4 * d + 4]


def home_kernel(got_ref, readout_ref, logprob_ref):
    rows, width = readout_ref.shape
    chunks = width // LANES
    per = chunks + 1
    pairs = got_ref.shape[0] // per
    info = jnp.concatenate([got_ref[per * d + chunks] for d in range(pairs)], axis=0)

    def left(x, n):
        return pltpu.roll(x, LANES - n, 1)

    info = info + left(info, 16) * (1.0 / 256.0) + left(info, 32) * (1.0 / 65536.0)
    tiles = [info[8 * t : 8 * t + 8] for t in range(pairs * rows // 8)]

    def fold(op, xs):
        x = functools.reduce(op, xs)
        return op(x, pltpu.roll(x, 4, 0))

    top = fold(jnp.maximum, tiles)
    total = fold(jnp.add, tiles)
    prods = [jnp.exp(x - top) * left(x, 1) for x in tiles]
    sums = fold(jnp.add, prods)
    coefs = [
        jnp.broadcast_to(p[:, 0:1] * jnp.exp2(x[:, 12:13]), (8, LANES)) for p, x in zip(prods, tiles)
    ]
    coefs = [coefs[d // 2][d % 2 * 4 : d % 2 * 4 + 4] for d in range(pairs)]
    inv = 1.0 / sums[:rows, 0:1]
    for k in range(chunks):
        acc = functools.reduce(jnp.add, [coefs[d] * got_ref[per * d + k] for d in range(pairs)])
        readout_ref[:, k * LANES : (k + 1) * LANES] = (acc * inv).astype(BF16)
    logprob_ref[...] = total[:rows, 4:12] - (top[:rows, 2:3] + jnp.log(sums[:rows, 2:3]))


def per_device(queries, centroids, leaves, beam):
    groups = lax.axis_size("cluster")
    rows, width = queries.shape
    count, leaf_count, _ = leaves.shape
    top = beam.shape[1]
    pairs = groups // 2
    half = pairs * rows
    total = 2 * half
    scale = 1.0 / math.sqrt(width)
    me = lax.axis_index("cluster")
    side = me % 2
    sides = [[2 * i + c for i in range(pairs)] for c in range(2)]
    swap = [(i, i ^ 1) for i in range(groups)]
    vmem = pl.BlockSpec(memory_space=pltpu.VMEM)

    hbm = pl.BlockSpec(memory_space=pltpu.HBM)
    leaves = lax.ppermute(leaves, "cluster", swap)

    spread = jnp.broadcast_to(queries[None], (pairs, rows, width))
    own = lax.all_to_all(spread, "cluster", 0, 0, axis_index_groups=sides)
    own, beam = lax.optimization_barrier((own, beam))
    other = lax.ppermute(own, "cluster", swap)
    slots = count * CAP
    disp, mine, mine_t, turned, centroids = pl.pallas_call(
        table_kernel,
        out_shape=(
            jax.ShapeDtypeStruct((slots, total), BF16),
            jax.ShapeDtypeStruct((2 * slots, half), BF16),
            jax.ShapeDtypeStruct((half, 4 * slots), BF16),
            jax.ShapeDtypeStruct((top, half), jnp.int32),
            jax.ShapeDtypeStruct(centroids.shape, BF16),
        ),
        in_specs=[hbm] * 2,
        out_specs=(vmem,) * 5,
        scratch_shapes=[pltpu.VMEM((top, total), jnp.int32), pltpu.SemaphoreType.DMA((2,))],
        compiler_params=pltpu.CompilerParams(vmem_limit_bytes=4 << 20),
        cost_estimate=pl.CostEstimate(flops=50_000_000, bytes_accessed=4 << 20, transcendentals=0),
        name="table",
    )(*(pltpu.with_memory_space_constraint(a, pltpu.HBM) for a in (beam.T, centroids)))
    pack, info = pl.pallas_call(
        functools.partial(leaf_kernel, scale),
        out_shape=(
            jax.ShapeDtypeStruct(((width // LANES + 1) * slots + count, LANES), F32),
            jax.ShapeDtypeStruct((count, half), F32),
        ),
        in_specs=[vmem] * 5,
        out_specs=(vmem, vmem),
        scratch_shapes=[pltpu.VMEM((total, width), BF16)],
        compiler_params=pltpu.CompilerParams(vmem_limit_bytes=24 << 20),
        name="leaf",
    )(own, other, disp, centroids, leaves)
    theirs = lax.ppermute(pack, "cluster", swap)
    per = width // LANES + 1
    packed = pl.pallas_call(
        merge_kernel,
        out_shape=jax.ShapeDtypeStruct((pairs * per, rows, LANES), F32),
        in_specs=[vmem] * 6,
        out_specs=vmem,
        compiler_params=pltpu.CompilerParams(vmem_limit_bytes=8 << 20),
        name="merge",
    )(pack, info, theirs, mine, mine_t, turned)
    packed = packed.astype(jnp.float16)
    got = lax.all_to_all(packed, "cluster", 0, 0, axis_index_groups=sides, tiled=True).astype(F32)
    return pl.pallas_call(
        home_kernel,
        out_shape=(jax.ShapeDtypeStruct((rows, width), BF16), jax.ShapeDtypeStruct((rows, top), F32)),
        in_specs=[vmem],
        out_specs=(vmem, vmem),
        compiler_params=pltpu.CompilerParams(vmem_limit_bytes=8 << 20),
        name="home",
    )(got)


def solution(mesh):
    return jax.shard_map(
        per_device,
        mesh=mesh,
        in_specs=(
            P(("query", "cluster"), None),
            P("cluster", None),
            P("cluster", None, None),
            P("query", None),
        ),
        out_specs=(P(("query", "cluster"), None), P(("query", "cluster"), None)),
        check_vma=False,
    )
```

```python
import functools
import math

import jax
import jax.numpy as jnp
from jax import lax
from jax.experimental import pallas as pl
from jax.experimental.pallas import tpu as pltpu
from jax.sharding import PartitionSpec as P

FLOOR = -30000.0
CAP = 8
LANES = 128
F32 = jnp.float32
BF16 = jnp.bfloat16


def dot(a, b, ca, cb):
    return lax.dot_general(a, b, (((ca,), (cb,)), ((), ())), preferred_element_type=F32)


def pieces(x):
    hi = x.astype(BF16)
    lo = (x - hi.astype(F32)).astype(BF16)
    return hi, lo


def table_kernel(beam_ref, cent_ref, disp_ref, mine_ref, mine_t_ref, turned_ref, cent_out, beam_buf, sems):
    count = cent_ref.shape[0]
    total = beam_ref.shape[1]
    half = total // 2
    rows = total // lax.axis_size("cluster")
    copies = [
        pltpu.make_async_copy(beam_ref, beam_buf, sems.at[0]),
        pltpu.make_async_copy(cent_ref, cent_out, sems.at[1]),
    ]
    for copy in copies:
        copy.start()
    me = lax.axis_index("cluster")
    square = (total, total)
    down, across = (lax.broadcasted_iota(jnp.int32, square, d) for d in range(2))
    upper = jnp.where(down <= across, 1.0, 0.0).astype(BF16)
    r = lax.broadcasted_iota(jnp.int32, (total, 1), 0)
    p, r = r // half, r % half
    source = (r // rows * 2 + (p + me) % 2) * rows + r % rows
    order = jnp.where(source == across, 1.0, 0.0).astype(BF16)
    copies[0].wait()
    beam = beam_buf[...]
    firsts = ((me + 1 - 2 * (me % 2)) * count, me * count)
    hits = [
        jnp.max(jnp.where(beam == first + c, 1.0, 0.0), axis=0, keepdims=True) for first in firsts for c in range(count)
    ]
    rank = dot(jnp.concatenate(hits, axis=0).astype(BF16), upper, 1, 0)
    slot = lax.broadcasted_iota(jnp.int32, (CAP, total), 0).astype(F32) + 1.0
    disp = jnp.concatenate(
        [jnp.where(slot == rank[c : c + 1], 1.0, 0.0) * hits[c] for c in range(2 * count)], axis=0
    ).astype(BF16)
    turned = dot(disp, order, 1, 1).astype(BF16)
    disp_ref[...] = turned[: count * CAP]
    mine_ref[...] = turned[:, :half]
    mine_t_ref[...] = dot(order[:half], jnp.concatenate([disp, disp], axis=0), 1, 1).astype(BF16)
    coarse = beam // 16 * 16
    halves = jnp.concatenate([coarse, beam - coarse], axis=0).astype(F32).astype(BF16)
    halves = dot(halves, order[:half], 1, 1)
    top = beam.shape[0]
    turned_ref[...] = (halves[:top] + halves[top:]).astype(jnp.int32)
    copies[1].wait()


def leaf_kernel(scale, own_ref, other_ref, disp_ref, cent_ref, leaves_ref, pack_ref, info_ref, q_ref):
    count, leaf_count, width = leaves_ref.shape
    pairs, rows, _ = own_ref.shape
    half = pairs * rows
    total = 2 * half
    for side, ref in enumerate((own_ref, other_ref)):
        for d in range(pairs):
            q_ref[side * half + d * rows : side * half + (d + 1) * rows] = ref[d]
    q = q_ref[...]
    disp = disp_ref[...]
    picked = dot(disp, q, 1, 0).astype(BF16)
    cs = dot(cent_ref[...], q, 1, 1) * scale
    def scores(c):
        return dot(picked[c * CAP : (c + 1) * CAP], leaves_ref[c], 1, 1)

    z = jnp.concatenate([scores(c) for c in range(count)], axis=0) * scale
    m = jnp.max(z, axis=1, keepdims=True)
    w = jnp.exp(z - m)
    l = jnp.sum(w, axis=1, keepdims=True)
    w = w.astype(BF16)
    accs = [dot(w[c * CAP : (c + 1) * CAP], leaves_ref[c], 1, 0) for c in range(count)]
    info_ref[...] = cs[:, :half]
    slots = count * CAP
    for c in range(count):
        for k in range(width // LANES):
            pack_ref[k * slots + c * CAP : k * slots + (c + 1) * CAP] = accs[c][:, k * LANES : (k + 1) * LANES]
    lane = lax.broadcasted_iota(jnp.int32, (slots, LANES), 1)
    base = width // LANES * slots
    pack_ref[base : base + slots] = jnp.where(
        lane == 0, m, l
    )
    pack_ref[base + slots :] = cs[:, half:]


def merge_kernel(pack_ref, info_ref, theirs_ref, mine_ref, mine_t_ref, beam_ref, out_ref):
    half = info_ref.shape[1]
    slots = mine_ref.shape[0] // 2
    count = info_ref.shape[0]
    chunks = (pack_ref.shape[0] - count) // slots - 1
    base = chunks * slots

    def both(k):
        return jnp.concatenate([ref[k * slots : (k + 1) * slots] for ref in (pack_ref, theirs_ref)], axis=0)

    stats = both(chunks)
    cs = jnp.concatenate([theirs_ref[base + slots :], info_ref[...]], axis=0)
    wide = jnp.concatenate([jnp.broadcast_to(cs[c : c + 1], (CAP, half)) for c in range(2 * count)], axis=0)
    on = mine_ref[...].astype(F32) > 0.5
    slot_m = stats[:, 0:1] + jnp.sum(jnp.where(on, wide, 0.0), axis=1, keepdims=True)
    slot_l = stats[:, 1:2]
    m = jnp.max(jnp.where(on, slot_m, FLOOR), axis=0, keepdims=True)
    back = jnp.sum(jnp.where(on, m, 0.0), axis=1, keepdims=True)
    f = jnp.exp(jnp.minimum(slot_m - back, 0.0))
    l = jnp.sum(jnp.where(on, f * slot_l, 0.0), axis=0, keepdims=True)
    mine_t = mine_t_ref[...]
    accs = []
    for k in range(chunks):
        hi, lo = pieces(f * both(k))
        accs.append(dot(mine_t, jnp.concatenate([hi, lo], axis=0), 1, 0))
    c = jnp.max(cs, axis=0, keepdims=True)
    cl = jnp.sum(jnp.exp(cs - c), axis=0, keepdims=True)
    me = lax.axis_index("cluster")
    firsts = ((me + 1 - 2 * (me % 2)) * count, me * count)
    beam = beam_ref[...]
    score = jnp.zeros(beam.shape, F32)
    for i in range(2 * count):
        score = score + jnp.where(beam == firsts[i // count] + i % count, cs[i : i + 1], 0.0)
    inv = 1.0 / jnp.maximum(l, 1e-30)
    info = jnp.concatenate([m, l, c, cl, score, jnp.zeros((4, half), F32)], axis=0)
    hi = info.astype(BF16).astype(F32)
    rest = info - hi
    mid = rest.astype(BF16).astype(F32)
    block = jnp.concatenate(
        [hi, mid * 256.0, (rest - mid) * 65536.0, inv, jnp.zeros((LANES - 49, half), F32)], axis=0
    )
    cols = block.T
    inv = cols[:, 48:49]
    outs = [acc * inv for acc in accs]
    high = jnp.max(functools.reduce(jnp.maximum, [jnp.abs(o) for o in outs]), axis=1, keepdims=True)
    power = jnp.floor(jnp.log2(jnp.maximum(high, 1e-30)))
    down = jnp.exp2(-power)
    lane = lax.broadcasted_iota(jnp.int32, (half, LANES), 1)
    cols = jnp.where(lane == 12, power, jnp.where(lane < 48, cols, 0.0))
    per = chunks + 1
    for k, value in enumerate([o * down for o in outs] + [cols]):
        for d in range(half // 4):
            out_ref[per * d + k] = value[4 * d : 4 * d + 4]


def home_kernel(got_ref, readout_ref, logprob_ref):
    rows, width = readout_ref.shape
    chunks = width // LANES
    per = chunks + 1
    pairs = got_ref.shape[0] // per
    info = jnp.concatenate([got_ref[per * d + chunks] for d in range(pairs)], axis=0)

    def left(x, n):
        return pltpu.roll(x, LANES - n, 1)

    info = info + left(info, 16) * (1.0 / 256.0) + left(info, 32) * (1.0 / 65536.0)
    tiles = [info[8 * t : 8 * t + 8] for t in range(pairs * rows // 8)]

    def fold(op, xs):
        x = functools.reduce(op, xs)
        return op(x, pltpu.roll(x, 4, 0))

    top = fold(jnp.maximum, tiles)
    total = fold(jnp.add, tiles)
    prods = [jnp.exp(x - top) * left(x, 1) for x in tiles]
    sums = fold(jnp.add, prods)
    coefs = [
        jnp.broadcast_to(p[:, 0:1] * jnp.exp2(x[:, 12:13]), (8, LANES)) for p, x in zip(prods, tiles)
    ]
    coefs = [coefs[d // 2][d % 2 * 4 : d % 2 * 4 + 4] for d in range(pairs)]
    inv = 1.0 / sums[:rows, 0:1]
    for k in range(chunks):
        acc = functools.reduce(jnp.add, [coefs[d] * got_ref[per * d + k] for d in range(pairs)])
        readout_ref[:, k * LANES : (k + 1) * LANES] = (acc * inv).astype(BF16)
    logprob_ref[...] = total[:rows, 4:12] - (top[:rows, 2:3] + jnp.log(sums[:rows, 2:3]))


def per_device(queries, centroids, leaves, beam):
    groups = lax.axis_size("cluster")
    rows, width = queries.shape
    count, leaf_count, _ = leaves.shape
    top = beam.shape[1]
    pairs = groups // 2
    half = pairs * rows
    total = 2 * half
    scale = 1.0 / math.sqrt(width)
    me = lax.axis_index("cluster")
    side = me % 2
    sides = [[2 * i + c for i in range(pairs)] for c in range(2)]
    swap = [(i, i ^ 1) for i in range(groups)]
    vmem = pl.BlockSpec(memory_space=pltpu.VMEM)

    hbm = pl.BlockSpec(memory_space=pltpu.HBM)
    leaves = lax.ppermute(leaves, "cluster", swap)

    spread = jnp.broadcast_to(queries[None], (pairs, rows, width))
    own = lax.all_to_all(spread, "cluster", 0, 0, axis_index_groups=sides)
    own, beam = lax.optimization_barrier((own, beam))
    other = lax.ppermute(own, "cluster", swap)
    slots = count * CAP
    disp, mine, mine_t, turned, centroids = pl.pallas_call(
        table_kernel,
        out_shape=(
            jax.ShapeDtypeStruct((slots, total), BF16),
            jax.ShapeDtypeStruct((2 * slots, half), BF16),
            jax.ShapeDtypeStruct((half, 4 * slots), BF16),
            jax.ShapeDtypeStruct((top, half), jnp.int32),
            jax.ShapeDtypeStruct(centroids.shape, BF16),
        ),
        in_specs=[hbm] * 2,
        out_specs=(vmem,) * 5,
        scratch_shapes=[pltpu.VMEM((top, total), jnp.int32), pltpu.SemaphoreType.DMA((2,))],
        compiler_params=pltpu.CompilerParams(vmem_limit_bytes=4 << 20),
        cost_estimate=pl.CostEstimate(flops=50_000_000, bytes_accessed=4 << 20, transcendentals=0),
        name="table",
    )(*(pltpu.with_memory_space_constraint(a, pltpu.HBM) for a in (beam.T, centroids)))
    pack, info = pl.pallas_call(
        functools.partial(leaf_kernel, scale),
        out_shape=(
            jax.ShapeDtypeStruct(((width // LANES + 1) * slots + count, LANES), F32),
            jax.ShapeDtypeStruct((count, half), F32),
        ),
        in_specs=[vmem] * 5,
        out_specs=(vmem, vmem),
        scratch_shapes=[pltpu.VMEM((total, width), BF16)],
        compiler_params=pltpu.CompilerParams(vmem_limit_bytes=24 << 20),
        name="leaf",
    )(own, other, disp, centroids, leaves)
    theirs = lax.ppermute(pack, "cluster", swap)
    per = width // LANES + 1
    packed = pl.pallas_call(
        merge_kernel,
        out_shape=jax.ShapeDtypeStruct((pairs * per, rows, LANES), F32),
        in_specs=[vmem] * 6,
        out_specs=vmem,
        compiler_params=pltpu.CompilerParams(vmem_limit_bytes=8 << 20),
        name="merge",
    )(pack, info, theirs, mine, mine_t, turned)
    packed = packed.astype(jnp.float16)
    got = lax.all_to_all(packed, "cluster", 0, 0, axis_index_groups=sides, tiled=True).astype(F32)
    return pl.pallas_call(
        home_kernel,
        out_shape=(jax.ShapeDtypeStruct((rows, width), BF16), jax.ShapeDtypeStruct((rows, top), F32)),
        in_specs=[vmem],
        out_specs=(vmem, vmem),
        compiler_params=pltpu.CompilerParams(vmem_limit_bytes=8 << 20),
        name="home",
    )(got)


def solution(mesh):
    return jax.shard_map(
        per_device,
        mesh=mesh,
        in_specs=(
            P(("query", "cluster"), None),
            P("cluster", None),
            P("cluster", None, None),
            P("query", None),
        ),
        out_specs=(P(("query", "cluster"), None), P(("query", "cluster"), None)),
        check_vma=False,
    )
```
